32 devices in a mesh: slide: 4 (over x, core), seq: 8 (over z, y).
Axes of the slice: x: 2, y: 2, z: 4, core: 2. Of those that a mesh axis runs over, the one named last changes fastest.
Arguments:
- tiles: bfloat16 [32768, 768], P(('slide', 'seq')), may hold values from -6 to 6
- route: int32 [32768], P(('slide', 'seq')), may hold values from 0 to 32767, as said below
- counts: int32 [4], replicated, may hold values from 2048 to 8192, as said below
- w_qkv: bfloat16 [768, 2304], replicated
- w_out: bfloat16 [768, 768], replicated, may hold values from -0.21875 to 0.21875
Outputs:
- mixed: bfloat16 [32768, 768], P(('slide', 'seq'))
The draws below stay inside these ranges and needn't reach their ends.
Inputs may be any that keep to these rules, and one draw needn't show every extreme that they name: `route`: every position of the 4 x 8192 sequences is named exactly once. The rows of one loader device (aligned blocks of 1024 rows) name either 16 or 48 positions in each aligned block of 1024 positions, and exactly 48 in some of them. `counts`: at least one slide is full.
All inputs are finite; a program needn't handle non-finite values.
Results may differ from the reference program's by a relative error of at most 0.0067.
Values may be sent and summed in bfloat16 or wider, within the bound.
A program may use at most 128 MiB of HBM per device.

```python
import jax
import jax.numpy as jnp
from jax import lax

D = 768
HEADS = 16
HEAD_DIM = 48
TOK_DEV = 1024
RATE_MID = 4
SLIDES = 4
CAP = 8192
LOADERS = 32
MOST = 48
N_SEQ = 8


def ranks_of(labels, owners):
    order = jnp.argsort(labels, stable=True)
    sorted_labels = labels[order]
    sizes = jnp.sum((labels[:, None] == jnp.arange(owners)[None, :]).astype(jnp.int32), 0)
    starts = jnp.cumsum(sizes) - sizes
    placed_rank = jnp.arange(labels.shape[0], dtype=jnp.int32) - starts[sorted_labels]
    return jnp.zeros_like(labels).at[order].set(placed_rank.astype(jnp.int32))


def draw_route(key, part):
    owners = LOADERS
    base = TOK_DEV // owners
    swing = base // 2
    key_roll, key_send, key_take = jax.random.split(jax.random.fold_in(key, 11), 3)
    roll = jax.random.randint(key_roll, (), 0, 2)
    index = jnp.arange(owners)
    parity = (index[None, :] - index[:, None] + roll) % 2
    amounts = base + swing * jnp.where(parity == 0, 1, -1)

    def labels_for(one_key, row):
        labels = jnp.repeat(index, row, total_repeat_length=TOK_DEV).astype(jnp.int32)
        return jax.random.permutation(one_key, labels)
    send_labels = jax.vmap(labels_for)(jax.random.split(key_send, owners), amounts)
    take_labels = jax.vmap(labels_for)(jax.random.split(key_take, owners), jnp.transpose(amounts))
    send_rank = jax.vmap(lambda labels: ranks_of(labels, owners))(send_labels)
    take_rank = jax.vmap(lambda labels: ranks_of(labels, owners))(take_labels)
    owner_index = jnp.broadcast_to(index[:, None], (owners, TOK_DEV))
    slot_index = jnp.broadcast_to(jnp.arange(TOK_DEV)[None, :], (owners, TOK_DEV))
    table = jnp.zeros((owners, owners, MOST), jnp.int32)
    table = table.at[owner_index, take_labels, take_rank].set(slot_index.astype(jnp.int32))
    source_index = jnp.broadcast_to(index[:, None], (owners, TOK_DEV))
    slots = table[send_labels, source_index, send_rank]
    return (send_labels * TOK_DEV + slots).reshape(owners * TOK_DEV).astype(jnp.int32)


def draw_counts(key, part):
    key_len, key_full = jax.random.split(jax.random.fold_in(key, 23))
    lengths = jax.random.randint(key_len, (SLIDES,), CAP // 4, CAP + 1)
    full = jax.random.randint(key_full, (), 0, SLIDES)
    return jnp.where(jnp.arange(SLIDES) == full, CAP, lengths).astype(jnp.int32)


def draw_w_qkv(key, part):
    key_base = jax.random.fold_in(jax.random.fold_in(key, 37), 0)
    base = jax.random.normal(key_base, (D, 3 * D), jnp.float32) * D ** (-0.5)
    return base.astype(jnp.bfloat16)


def block_scale(key, dims, cuts, smallest, largest):
    loudness = 1.0
    for position, shards_of in cuts:
        steps = jax.random.uniform(jax.random.fold_in(jax.random.fold_in(key, 6), position), (shards_of,), jnp.float32, smallest / len(cuts), largest / len(cuts))
        loudness = loudness * jnp.repeat(jnp.exp(steps), dims[position] // shards_of).reshape((-1,) + (1,) * (len(dims) - 1 - position))
    return loudness


def normal_values(own_key, dims, width, most, cuts=(), kind=jnp.bfloat16):
    values = jax.random.normal(own_key, dims, jnp.float32) * width
    if len(cuts) > 0:
        values = block_scale(own_key, dims, cuts, -0.22, 0.18) * values
    return jnp.clip(values, min=-most, max=most).astype(kind)


def setup_inputs(seed: int = 0) -> dict:
    seeds = jax.random.split(jax.random.key(seed), 6)
    tiles = normal_values(seeds[0], (SLIDES * CAP, D), 1.0, 6.0, ((0, 32),))
    route = draw_route(jax.random.fold_in(seeds[5], 71), 0)
    counts = draw_counts(jax.random.fold_in(seeds[5], 71), 0)
    w_qkv = draw_w_qkv(jax.random.fold_in(seeds[5], 71), 0)
    w_out = normal_values(seeds[4], (D, D), D ** -0.5, 0.21875)
    return {"tiles": tiles, "route": route, "counts": counts, "w_qkv": w_qkv, "w_out": w_out}


def layer_norm(values):
    mean = lax.optimization_barrier(jnp.mean(values, -1, keepdims=True))
    centred = values - mean
    var = lax.optimization_barrier(jnp.mean(centred * centred, -1, keepdims=True))
    return centred * lax.rsqrt(var + 1e-05)

def attend(query, keys, values, key_valid):
    scale = 1.0 / HEAD_DIM ** 0.5
    rows = query.shape[0]
    block = min(512, rows)
    keys_wide = keys.astype(jnp.float32)
    values_wide = values.astype(jnp.float32)
    mask = jnp.transpose(key_valid)[:, None, :]

    def one_block(query_block):
        scores = jnp.einsum('qhd,khd->hqk', query_block.astype(jnp.float32), keys_wide) * scale
        scores = jnp.where(mask, scores, -1e+30)
        top = lax.optimization_barrier(jnp.max(scores, -1))
        weights = jnp.where(mask, jnp.exp(scores - top[..., None]), 0.0)
        total = lax.optimization_barrier(jnp.sum(weights, -1))
        rounded = lax.optimization_barrier(weights.astype(jnp.bfloat16)).astype(jnp.float32)
        result = jnp.einsum('hqk,khd->qhd', rounded, values_wide)
        return (result, jnp.transpose(top), jnp.transpose(total))
    blocks = query.reshape(rows // block, block, HEADS, HEAD_DIM)
    result, top, total = lax.map(one_block, blocks)
    return (result.reshape(rows, HEADS, HEAD_DIM), top.reshape(rows, HEADS), total.reshape(rows, HEADS))

def picker(rate):
    return jnp.arange(HEADS)[None, :] % rate == jnp.arange(rate)[:, None]

def select(array, rate):
    pick = picker(rate).astype(array.dtype)
    shaped = array.reshape(array.shape[0] // rate, rate, HEADS, HEAD_DIM)
    return lax.optimization_barrier(jnp.sum(shaped * pick[None, :, :, None], 1)).astype(array.dtype)

def spread(result, top, total, rate):
    pick = picker(rate)
    count_rows = result.shape[0] * rate
    full = (result[:, None] * pick[None, :, :, None].astype(jnp.float32)).reshape(count_rows, HEADS, HEAD_DIM)
    top_full = jnp.where(pick[None], top[:, None, :], -1e+30).reshape(count_rows, HEADS)
    total_full = (total[:, None, :] * pick[None].astype(jnp.float32)).reshape(count_rows, HEADS)
    return (full, top_full, total_full)

def level(query, keys, values, count, segment, rate):
    taken = CAP // rate
    nseg = CAP // segment
    sub = segment // rate
    positions = jnp.arange(taken)[:, None] * rate + (jnp.arange(HEADS) % rate)[None, :]
    key_valid = positions < count
    pieces = (select(query, rate).reshape(nseg, sub, HEADS, HEAD_DIM), select(keys, rate).reshape(nseg, sub, HEADS, HEAD_DIM), select(values, rate).reshape(nseg, sub, HEADS, HEAD_DIM), key_valid.reshape(nseg, sub, HEADS))
    result, top, total = lax.map(lambda item: attend(item[0], item[1], item[2], item[3]), pieces)
    return spread(result.reshape(taken, HEADS, HEAD_DIM), top.reshape(taken, HEADS), total.reshape(taken, HEADS), rate)

def one_slide(item, w_qkv, w_out):
    placed, count = item
    valid = jnp.arange(CAP) < count
    normed = layer_norm(placed.astype(jnp.float32)).astype(jnp.bfloat16)
    qkv = jnp.dot(normed, w_qkv, preferred_element_type=jnp.float32).astype(jnp.bfloat16)
    qkv = qkv.reshape(CAP, 3, HEADS, HEAD_DIM)
    query, keys, values = (qkv[:, 0], qkv[:, 1], qkv[:, 2])
    levels = [level(query, keys, values, count, TOK_DEV // 2, 1), level(query, keys, values, count, RATE_MID * TOK_DEV, RATE_MID), level(query, keys, values, count, CAP, N_SEQ)]
    highest = jnp.maximum(jnp.maximum(levels[0][1], levels[1][1]), levels[2][1])
    numer = jnp.zeros((CAP, HEADS, HEAD_DIM), jnp.float32)
    denom = jnp.zeros((CAP, HEADS), jnp.float32)
    for result, top, total in levels:
        factor = jnp.exp(top - highest)
        numer = numer + factor[..., None] * result
        denom = denom + factor * total
    denom = jnp.where(valid[:, None], denom, 1.0)
    attended = jnp.where(valid[:, None, None], numer / denom[..., None], 0.0)
    attended = attended.reshape(CAP, D).astype(jnp.bfloat16)
    projected = jnp.dot(attended, w_out, preferred_element_type=jnp.float32)
    mixed = placed.astype(jnp.float32) + layer_norm(projected)
    return jnp.where(valid[:, None], mixed, 0.0).astype(jnp.bfloat16)

def reference(tiles, route, counts, w_qkv, w_out):
    placed = jnp.zeros((SLIDES * CAP, D), jnp.bfloat16).at[route].set(tiles)
    placed = placed.reshape(SLIDES, CAP, D)
    mixed = lax.map(lambda item: one_slide(item, w_qkv, w_out), (placed, counts))
    return mixed.reshape(SLIDES * CAP, D)
```

```python
import functools
import math

import jax
import jax.numpy as jnp
from jax import lax
from jax.experimental import pallas as pl
from jax.experimental.pallas import tpu as pltpu
from jax.sharding import PartitionSpec as P

HEADS = 16
RATE_MID = 4
PAIRS = HEADS // 2
LANES = 128
NT = (((1,), (1,)), ((), ()))
BF = jnp.bfloat16
F32 = jnp.float32


def iota(shape, dim):
    return lax.broadcasted_iota(jnp.int32, shape, dim)


def dot(a, b):
    return jnp.dot(a, b, preferred_element_type=F32)


def dot_nt(a, b):
    return lax.dot_general(a, b, NT, preferred_element_type=F32)


def position_of(row, rows, n_seq):
    half = rows // 2
    run = half // n_seq
    seg = row // half
    block = (row % half) // run
    index = row % run
    group = n_seq // RATE_MID
    residue = (block % group) * RATE_MID + block // group
    return seg * half + index * n_seq + residue


def row_of(position, rows, n_seq):
    half = rows // 2
    run = half // n_seq
    seg = position // half
    within = position % half
    residue = within % n_seq
    block = (residue % RATE_MID) * (n_seq // RATE_MID) + residue // RATE_MID
    return seg * half + block * run + within // n_seq


def block_of(residue, n_seq):
    return (residue % RATE_MID) * (n_seq // RATE_MID) + residue // RATE_MID


def layer_norm(values):
    mean = jnp.mean(values, -1, keepdims=True)
    centred = values - mean
    var = jnp.mean(centred * centred, -1, keepdims=True)
    return centred * lax.rsqrt(var + 1e-05)


def dispatch_kernel(owners, most, n_seq, route_ref, tiles_ref, out_ref, places_ref):
    rows = tiles_ref.shape[0]
    slots = owners * most
    route = route_ref[...]
    target = route // rows
    local = row_of(route % rows, rows, n_seq)
    mine = iota((owners, rows), 0) == target
    upper = (iota((rows, rows), 0) <= iota((rows, rows), 1)).astype(BF)
    counted = dot(mine.astype(BF), upper)
    rank = jnp.sum(jnp.where(mine, counted, 0.0), 0, keepdims=True).astype(jnp.int32) - 1
    slot = target * most + rank
    move = (iota((slots, rows), 0) == slot).astype(BF)
    out_ref[...] = dot(move, tiles_ref[...]).astype(BF)
    kind = iota((8, rows), 0)
    digits = jnp.where(
        kind == 0, local // 32, jnp.where(kind == 1, local % 32, jnp.where(kind == 2, 1, 0))
    )
    sent = dot_nt(digits.astype(F32).astype(BF), move)
    place = sent[0:1] * 32.0 + sent[1:2] + (1.0 - sent[2:3]) * (2.0 * rows)
    places_ref[...] = place.astype(jnp.int32)


def project_kernel(n_seq, limit_ref, land_ref, arrived_ref, w_ref, placed_ref, q_ref, k_ref,
                   v_ref, mid_ref, wide_ref):
    rows = placed_ref.shape[0]
    half = rows // 2
    run = half // n_seq
    slots = arrived_ref.shape[0]
    take = (iota((rows, slots), 0) == land_ref[...]).astype(BF)
    placed = dot(take, arrived_ref[...])
    placed_ref[...] = placed.astype(BF)
    normed = layer_norm(placed).astype(BF)
    lane = iota((rows, LANES), 1)
    position = position_of(iota((rows, LANES), 0), rows, n_seq)
    valid = position < limit_ref[0]
    flag = (lane == 96) | (lane == 97)
    ones = jnp.where(flag, 1.0, 0.0)
    bias = jnp.where(flag & jnp.logical_not(valid), -1e30, 0.0)
    width = PAIRS * LANES
    small_lane = iota((run, LANES), 1)
    first = (small_lane < 48) | (small_lane == 96)
    for pair in range(PAIRS):
        for part, (ref, extra) in enumerate(((q_ref, ones), (k_ref, bias), (v_ref, ones))):
            start = part * width + pair * LANES
            value = (dot(normed, w_ref[:, start : start + LANES]) + extra).astype(BF)
            ref[pair] = value
            if part > 0:
                step = half // RATE_MID
                for seg in range(2):
                    base = seg * half + (pair % RATE_MID) * step
                    mid_ref[part - 1, pair, seg * step : (seg + 1) * step] = value[
                        base : base + step
                    ]
                    base_a = seg * half + block_of(pair % n_seq, n_seq) * run
                    base_b = seg * half + block_of((pair + PAIRS) % n_seq, n_seq) * run
                    wide = value[base_a : base_a + run]
                    if base_a != base_b:
                        wide = jnp.where(first, wide, value[base_b : base_b + run])
                    wide_ref[part - 1, pair, seg * run : (seg + 1) * run] = wide


def one_head(query, keys, values, head, factor):
    lane = iota(query.shape, 1)
    own = ((lane >= 48 * head) & (lane < 48 * head + 48)) | (lane == 96 + head)
    query = jnp.where(own, query, jnp.zeros_like(query))
    scores = dot_nt(query, keys)
    top = jnp.max(scores, -1, keepdims=True)
    weights = jnp.exp2((scores - top) * factor).astype(BF)
    return dot(weights, values), top


def near_kernel(factor, q_ref, k_ref, v_ref, out_ref):
    rows = q_ref.shape[1]
    half = rows // 2
    block = 256
    for seg in range(2):
        keys = k_ref[0, seg * half : (seg + 1) * half]
        values = v_ref[0, seg * half : (seg + 1) * half]
        for start in range(seg * half, (seg + 1) * half, block):
            query = q_ref[0, start : start + block]
            result_a, top_a = one_head(query, keys, values, 0, factor)
            result_b, top_b = one_head(query, keys, values, 1, factor)
            lane = iota(result_a.shape, 1)
            own_a = (lane < 48) | (lane == 96)
            packed = jnp.where(own_a, result_a, result_b)
            packed = jnp.where(lane == 98, top_a, packed)
            packed = jnp.where(lane == 99, top_b, packed)
            out_ref[0, start : start + block] = packed


def far_kernel(n_seq, factor, limit_ref, q_ref, near_ref, mid_ref, wide_ref, w_ref, placed_ref,
               out_ref, att_ref):
    pair = pl.program_id(0)
    rows = q_ref.shape[1]
    half = rows // 2
    run = half // n_seq
    step = half // RATE_MID
    mid_base = lax.rem(pair, RATE_MID) * step

    def finish(result, total):
        return result * (1.0 / total)

    def aligned(base, size):
        return pl.multiple_of(base, size)

    near = near_ref[0]
    lane = iota(near.shape, 1)
    total = jnp.where(lane < 48, near[:, 96:97], near[:, 97:98])
    att_ref[pair] = jnp.where(lane < 96, finish(near, total), 0.0).astype(BF)

    mid_rows = [pl.ds(aligned(seg * half + mid_base, step), step) for seg in range(2)]
    query = jnp.concatenate([q_ref[0, part] for part in mid_rows], 0)
    local = jnp.concatenate([near_ref[0, part] for part in mid_rows], 0)
    mid_count = mid_ref.shape[0] * mid_ref.shape[3]
    mid_keys = mid_ref[:, 0, 0].reshape(mid_count, LANES)
    mid_values = mid_ref[:, 1, 0].reshape(mid_count, LANES)
    wide_count = wide_ref.shape[0] * wide_ref.shape[3]
    wide_keys = wide_ref[:, 0, 0].reshape(wide_count, LANES)
    wide_values = wide_ref[:, 1, 0].reshape(wide_count, LANES)
    group = n_seq // RATE_MID
    merged = []
    for head in range(2):
        sum_mid, top_mid = one_head(query, mid_keys, mid_values, head, factor)
        residue = lax.rem(pair + head * PAIRS, n_seq)
        inner = residue // RATE_MID
        wide_rows = [
            pl.ds(aligned(seg * half + mid_base + inner * run, run), run) for seg in range(2)
        ]
        wide_query = jnp.concatenate([q_ref[0, part] for part in wide_rows], 0)
        sum_wide, top_wide = one_head(wide_query, wide_keys, wide_values, head, factor)
        zero = jnp.zeros((run, LANES), F32)
        low = jnp.full((run, 1), -1e30, F32)
        sums, tops = [], []
        for seg in range(2):
            piece = sum_wide[seg * run : (seg + 1) * run]
            piece_top = top_wide[seg * run : (seg + 1) * run]
            for index in range(group):
                sums.append(jnp.where(inner == index, piece, zero))
                tops.append(jnp.where(inner == index, piece_top, low))
        sum_wide = jnp.concatenate(sums, 0)
        top_wide = jnp.concatenate(tops, 0)
        top_near = local[:, 98 + head : 99 + head]
        top = jnp.maximum(jnp.maximum(top_near, top_mid), top_wide)
        numer = (
            local * jnp.exp2((top_near - top) * factor)
            + sum_mid * jnp.exp2((top_mid - top) * factor)
            + sum_wide * jnp.exp2((top_wide - top) * factor)
        )
        merged.append(finish(numer, numer[:, 96 + head : 97 + head]))
    lane = iota(merged[0].shape, 1)
    both = jnp.where(lane < 48, merged[0], jnp.where(lane < 96, merged[1], 0.0)).astype(BF)
    for seg in range(2):
        att_ref[pair, mid_rows[seg]] = both[seg * step : (seg + 1) * step]

    @pl.when(pair == PAIRS - 1)
    def _():
        limit = limit_ref[0]
        row = iota((half, half), 1)
        want = iota((half, half), 0)
        unsort = (row_of(want, rows, n_seq) == row).astype(BF)
        for seg in range(2):
            part = slice(seg * half, (seg + 1) * half)
            projected = dot(att_ref[0, part], w_ref[:LANES])
            for other in range(1, PAIRS):
                projected += dot(
                    att_ref[other, part], w_ref[other * LANES : (other + 1) * LANES]
                )
            mixed = placed_ref[part].astype(F32) + layer_norm(projected)
            position = iota(mixed.shape, 0) + seg * half
            mixed = dot(unsort, mixed.astype(BF))
            out_ref[part] = jnp.where(position < limit, mixed, 0.0).astype(BF)


def body(tiles, route, counts, w_qkv, w_out):
    rows, width = tiles.shape
    n_slide = lax.axis_size("slide")
    n_seq = lax.axis_size("seq")
    owners = n_slide * n_seq
    most = 3 * rows // (2 * owners)
    slots = owners * most
    head_dim = width // HEADS
    factor = math.log2(math.e) / math.sqrt(head_dim)
    padded = PAIRS * LANES
    vmem = pl.BlockSpec(memory_space=pltpu.VMEM)
    smem = pl.BlockSpec(memory_space=pltpu.SMEM)
    big = pltpu.CompilerParams(vmem_limit_bytes=48 << 20)

    outgoing, places = pl.pallas_call(
        functools.partial(dispatch_kernel, owners, most, n_seq),
        out_shape=(
            jax.ShapeDtypeStruct((slots, width), BF),
            jax.ShapeDtypeStruct((1, slots), jnp.int32),
        ),
        in_specs=[vmem, vmem],
        out_specs=(vmem, vmem),
        compiler_params=big,
        name="dispatch",
    )(route.reshape(1, rows), tiles)
    exchange = functools.partial(
        lax.all_to_all, axis_name=("slide", "seq"), split_axis=0, concat_axis=0, tiled=True
    )
    landing = exchange(places.reshape(owners, most)).reshape(1, slots)
    arrived = exchange(outgoing.reshape(owners, most, width)).reshape(slots, width)

    column = jnp.arange(padded)
    lane = column % LANES
    source = (column // LANES + PAIRS * (lane // head_dim)) * head_dim + lane % head_dim
    source = jnp.where(lane < 2 * head_dim, source, -1)
    pick = (jnp.arange(width)[:, None] == source[None, :]).astype(BF)
    w_in = jnp.concatenate(
        [dot(w_qkv[:, i * width : (i + 1) * width], pick).astype(BF) for i in range(3)], 1
    )
    w_back = lax.dot_general(
        pick, w_out, (((0,), (0,)), ((), ())), preferred_element_type=F32
    ).astype(BF)

    seq_index = lax.axis_index("seq")
    limit = (counts[lax.axis_index("slide")] - seq_index * rows).reshape(1)
    heads_shape = jax.ShapeDtypeStruct((PAIRS, rows, LANES), BF)
    mid_taken, wide_taken = rows // RATE_MID, rows // n_seq
    placed, query, keys, values, mid_local, wide_local = pl.pallas_call(
        functools.partial(project_kernel, n_seq),
        out_shape=(
            jax.ShapeDtypeStruct((rows, width), BF),
            heads_shape,
            heads_shape,
            heads_shape,
            jax.ShapeDtypeStruct((2, PAIRS, mid_taken, LANES), BF),
            jax.ShapeDtypeStruct((2, PAIRS, wide_taken, LANES), BF),
        ),
        in_specs=[smem, vmem, vmem, vmem],
        out_specs=(vmem,) * 6,
        compiler_params=big,
        name="project",
    )(limit, landing, arrived, w_in)

    groups = [
        [start + i for i in range(RATE_MID)] for start in range(0, n_seq, RATE_MID)
    ]
    mid_all = lax.all_gather(mid_local, "seq", axis_index_groups=groups)
    wide_all = lax.all_gather(wide_local, "seq")

    pair_spec = pl.BlockSpec((1, rows, LANES), lambda i: (i, 0, 0))
    near = pl.pallas_call(
        functools.partial(near_kernel, factor),
        out_shape=jax.ShapeDtypeStruct((PAIRS, rows, LANES), F32),
        grid=(PAIRS,),
        in_specs=[pair_spec] * 3,
        out_specs=pair_spec,
        compiler_params=big,
        cost_estimate=pl.CostEstimate(
            flops=4 * HEADS * rows * rows // 2 * LANES,
            bytes_accessed=10 * rows * padded,
            transcendentals=HEADS * rows * rows // 2,
        ),
        name="near",
    )(query, keys, values)

    whole = lambda shape: pl.BlockSpec(shape, lambda i: (0,) * len(shape))
    return pl.pallas_call(
        functools.partial(far_kernel, n_seq, factor),
        out_shape=jax.ShapeDtypeStruct((rows, width), BF),
        grid=(PAIRS,),
        in_specs=[
            smem,
            pair_spec,
            pair_spec,
            pl.BlockSpec((RATE_MID, 2, 1, mid_taken, LANES), lambda i: (0, 0, i, 0, 0)),
            pl.BlockSpec((n_seq, 2, 1, wide_taken, LANES), lambda i: (0, 0, i, 0, 0)),
            whole((padded, width)),
            whole((rows, width)),
        ],
        out_specs=whole((rows, width)),
        scratch_shapes=[pltpu.VMEM((PAIRS, rows, LANES), BF)],
        compiler_params=big,
        name="far",
    )(limit, query, near, mid_all, wide_all, w_back, placed)


def solution(mesh):
    return jax.shard_map(
        body,
        mesh=mesh,
        in_specs=(P(("slide", "seq"), None), P(("slide", "seq")), P(), P(), P()),
        out_specs=P(("slide", "seq"), None),
        check_vma=False,
    )
```

```python
import functools
import math

import jax
import jax.numpy as jnp
from jax import lax
from jax.experimental import pallas as pl
from jax.experimental.pallas import tpu as pltpu
from jax.sharding import PartitionSpec as P

HEADS = 16
RATE_MID = 4
PAIRS = HEADS // 2
LANES = 128
NT = (((1,), (1,)), ((), ()))
BF = jnp.bfloat16
F32 = jnp.float32


def iota(shape, dim):
    return lax.broadcasted_iota(jnp.int32, shape, dim)


def dot(a, b):
    return jnp.dot(a, b, preferred_element_type=F32)


def dot_nt(a, b):
    return lax.dot_general(a, b, NT, preferred_element_type=F32)


def position_of(row, rows, n_seq):
    half = rows // 2
    run = half // n_seq
    seg = row // half
    block = (row % half) // run
    index = row % run
    group = n_seq // RATE_MID
    residue = (block % group) * RATE_MID + block // group
    return seg * half + index * n_seq + residue


def row_of(position, rows, n_seq):
    half = rows // 2
    run = half // n_seq
    seg = position // half
    within = position % half
    residue = within % n_seq
    block = (residue % RATE_MID) * (n_seq // RATE_MID) + residue // RATE_MID
    return seg * half + block * run + within // n_seq


def block_of(residue, n_seq):
    return (residue % RATE_MID) * (n_seq // RATE_MID) + residue // RATE_MID


def layer_norm(values):
    mean = jnp.mean(values, -1, keepdims=True)
    centred = values - mean
    var = jnp.mean(centred * centred, -1, keepdims=True)
    return centred * lax.rsqrt(var + 1e-05)


def dispatch_kernel(owners, most, route_ref, tiles_ref, out_ref):
    rows = tiles_ref.shape[0]
    slots = owners * most
    target = route_ref[...] // rows
    mine = iota((owners, rows), 0) == target
    upper = (iota((rows, rows), 0) <= iota((rows, rows), 1)).astype(BF)
    counted = dot(mine.astype(BF), upper)
    rank = jnp.sum(jnp.where(mine, counted, 0.0), 0, keepdims=True).astype(jnp.int32) - 1
    slot = target * most + rank
    move = (iota((slots, rows), 0) == slot).astype(BF)
    out_ref[...] = dot(move, tiles_ref[...]).astype(BF)


def landing_kernel(most, n_seq, me_ref, routes_ref, out_ref):
    owners, rows = routes_ref.shape
    routes = routes_ref[...]
    mine = routes // rows == me_ref[0]
    local = row_of(routes % rows, rows, n_seq)
    upper = (iota((rows, rows), 0) <= iota((rows, rows), 1)).astype(BF)
    counted = dot(mine.astype(BF), upper).astype(jnp.int32)
    rank = jnp.where(mine, counted - 1, -1)
    high = (local // 32).astype(F32)
    low = (local % 32).astype(F32)
    kind = iota((8, rows), 0)
    for source in range(owners):
        part = slice(source, source + 1)
        onehot = (iota((most, rows), 0) == rank[part]).astype(BF)
        digits = jnp.where(kind == 0, high[part], jnp.where(kind == 1, low[part], 1.0))
        sent = dot_nt(digits.astype(BF), onehot)
        place = sent[0:1] * 32.0 + sent[1:2] + (1.0 - sent[2:3]) * (2.0 * rows)
        out_ref[part] = place.astype(jnp.int32)


def project_kernel(n_seq, limit_ref, land_ref, arrived_ref, w_ref, placed_ref, q_ref, k_ref,
                   v_ref, mid_ref, wide_ref):
    rows = placed_ref.shape[0]
    half = rows // 2
    run = half // n_seq
    step = half // RATE_MID
    slots = arrived_ref.shape[0]
    take = (iota((rows, slots), 0) == land_ref[...]).astype(BF)
    placed = dot(take, arrived_ref[...])
    placed_ref[...] = placed.astype(BF)
    normed = layer_norm(placed).astype(BF)
    lane = iota((rows, 2 * LANES), 1) % LANES
    position = position_of(iota((rows, 2 * LANES), 0), rows, n_seq)
    valid = position < limit_ref[0]
    flag = (lane == 96) | (lane == 97)
    ones = jnp.where(flag, 1.0, 0.0)
    bias = jnp.where(flag & jnp.logical_not(valid), -1e30, 0.0)
    width = PAIRS * LANES
    for couple in range(0, PAIRS, 2):
        for part, (ref, extra) in enumerate(((q_ref, ones), (k_ref, bias), (v_ref, ones))):
            start = part * width + couple * LANES
            both = (dot(normed, w_ref[:, start : start + 2 * LANES]) + extra).astype(BF)
            for pair in (couple, couple + 1):
                value = both[:, (pair - couple) * LANES : (pair - couple + 1) * LANES]
                ref[pair] = value
                for seg in range(2):
                    owner = pair % RATE_MID
                    base = seg * half + owner * step
                    mid_ref[owner, pair // RATE_MID, part, seg * step : (seg + 1) * step] = (
                        value[base : base + step]
                    )
                    for residue in range(pair, n_seq, PAIRS):
                        base = seg * half + block_of(residue, n_seq) * run
                        wide_ref[residue, part, seg * run : (seg + 1) * run] = value[
                            base : base + run
                        ]


def one_head(query, keys, values, head, factor):
    lane = iota(query.shape, 1)
    own = ((lane >= 48 * head) & (lane < 48 * head + 48)) | (lane == 96 + head)
    query = jnp.where(own, query, jnp.zeros_like(query))
    scores = dot_nt(query, keys)
    top = jnp.max(scores, -1, keepdims=True)
    weights = jnp.exp2((scores - top) * factor).astype(BF)
    result = dot(weights, values)
    total = result[:, 96:97]
    return result * (1.0 / total), top * factor + jnp.log2(total)


def near_kernel(factor, q_ref, k_ref, v_ref, out_ref):
    rows = q_ref.shape[1]
    half = rows // 2
    block = 256
    for seg in range(2):
        keys = k_ref[0, seg * half : (seg + 1) * half]
        values = v_ref[0, seg * half : (seg + 1) * half]
        for start in range(seg * half, (seg + 1) * half, block):
            query = q_ref[0, start : start + block]
            result_a, log_a = one_head(query, keys, values, 0, factor)
            result_b, log_b = one_head(query, keys, values, 1, factor)
            lane = iota(result_a.shape, 1)
            packed = jnp.where(lane < 48, result_a, result_b)
            packed = jnp.where(lane == 96, log_a, packed)
            packed = jnp.where(lane == 97, log_b, packed)
            out_ref[0, start : start + block] = packed


def pieces(value):
    first = value.astype(BF).astype(F32)
    second = (value - first).astype(BF).astype(F32)
    return first, second, value - first - second


def far_kernel(factor, ref, out_ref):
    count, taken = ref.shape[0], ref.shape[3]
    total = count * taken
    keys = ref[:, 0, 1].reshape(total, LANES)
    values = ref[:, 0, 2].reshape(total, LANES)
    for source in range(count):
        query = ref[source, 0, 0]
        result_a, log_a = one_head(query, keys, values, 0, factor)
        result_b, log_b = one_head(query, keys, values, 1, factor)
        lane = iota(result_a.shape, 1)
        packed = jnp.where(lane < 48, result_a, result_b)
        for index, piece in enumerate(pieces(log_a) + pieces(log_b)):
            packed = jnp.where(lane == 96 + index, piece, packed)
        out_ref[source, 0] = packed.astype(BF)


def merge_kernel(n_seq, limit_ref, near_ref, mid_ref, wide_ref, w_ref, placed_ref, out_ref,
                 att_ref):
    rows = placed_ref.shape[0]
    half = rows // 2
    run = half // n_seq
    step = half // RATE_MID
    group = n_seq // RATE_MID

    def log_of(packed, head):
        at = 96 + 3 * head
        return packed[:, at : at + 1] + packed[:, at + 1 : at + 2] + packed[:, at + 2 : at + 3]

    for pair in range(PAIRS):
        near_all = near_ref[pair]
        lane = iota(near_all.shape, 1)
        att_ref[pair] = jnp.where(lane < 96, near_all, 0.0).astype(BF)
        mid_all = mid_ref[pair % RATE_MID, pair // RATE_MID].astype(F32)
        lane = iota((run, LANES), 1)
        for seg in range(2):
            base = seg * half + (pair % RATE_MID) * step
            for index in range(group):
                part = slice(base + index * run, base + (index + 1) * run)
                near = near_ref[pair, part]
                at = seg * step + index * run
                mid = mid_all[at : at + run]
                merged = []
                for head in range(2):
                    residue = (pair + head * PAIRS) % n_seq
                    log_near, log_mid = near[:, 96 + head : 97 + head], log_of(mid, head)
                    top = jnp.maximum(log_near, log_mid)
                    has_wide = residue // RATE_MID == index
                    if has_wide:
                        wide = wide_ref[residue, seg * run : (seg + 1) * run].astype(F32)
                        log_wide = log_of(wide, head)
                        top = jnp.maximum(top, log_wide)
                    weight_near, weight_mid = jnp.exp2(log_near - top), jnp.exp2(log_mid - top)
                    numer = near * weight_near + mid * weight_mid
                    denom = weight_near + weight_mid
                    if has_wide:
                        weight_wide = jnp.exp2(log_wide - top)
                        numer += wide * weight_wide
                        denom += weight_wide
                    merged.append(numer * (1.0 / denom))
                both = jnp.where(lane < 48, merged[0], jnp.where(lane < 96, merged[1], 0.0))
                att_ref[pair, part] = both.astype(BF)

    limit = limit_ref[0]
    unsort = (row_of(iota((half, half), 0), rows, n_seq) == iota((half, half), 1)).astype(BF)
    for seg in range(2):
        part = slice(seg * half, (seg + 1) * half)
        attended = jnp.concatenate([att_ref[pair, part] for pair in range(PAIRS)], 1)
        projected = dot(attended, w_ref[...])
        mixed = placed_ref[part].astype(F32) + layer_norm(projected)
        position = iota(mixed.shape, 0) + seg * half
        mixed = dot(unsort, mixed.astype(BF))
        out_ref[part] = jnp.where(position < limit, mixed, 0.0).astype(BF)


def body(tiles, route, counts, w_qkv, w_out):
    rows, width = tiles.shape
    n_slide = lax.axis_size("slide")
    n_seq = lax.axis_size("seq")
    owners = n_slide * n_seq
    most = 3 * rows // (2 * owners)
    slots = owners * most
    head_dim = width // HEADS
    factor = math.log2(math.e) / math.sqrt(head_dim)
    padded = PAIRS * LANES
    vmem = pl.BlockSpec(memory_space=pltpu.VMEM)
    smem = pl.BlockSpec(memory_space=pltpu.SMEM)
    big = pltpu.CompilerParams(vmem_limit_bytes=48 << 20)

    seq_index = lax.axis_index("seq")
    slide_index = lax.axis_index("slide")
    both_axes = ("slide", "seq")
    routes = lax.all_gather(route, both_axes)
    outgoing = pl.pallas_call(
        functools.partial(dispatch_kernel, owners, most),
        out_shape=jax.ShapeDtypeStruct((slots, width), BF),
        in_specs=[vmem, vmem],
        out_specs=vmem,
        compiler_params=big,
        name="dispatch",
    )(route.reshape(1, rows), tiles)
    exchange = functools.partial(lax.all_to_all, split_axis=0, concat_axis=0, tiled=True)
    arrived = exchange(outgoing.reshape(owners, most, width), both_axes).reshape(slots, width)
    landing = pl.pallas_call(
        functools.partial(landing_kernel, most, n_seq),
        out_shape=jax.ShapeDtypeStruct((owners, most), jnp.int32),
        in_specs=[smem, vmem],
        out_specs=vmem,
        compiler_params=big,
        name="landing",
    )((slide_index * n_seq + seq_index).reshape(1), routes.reshape(owners, rows))
    landing = landing.reshape(1, slots)

    column = jnp.arange(padded)
    lane = column % LANES
    source = (column // LANES + PAIRS * (lane // head_dim)) * head_dim + lane % head_dim
    source = jnp.where(lane < 2 * head_dim, source, -1)
    pick = (jnp.arange(width)[:, None] == source[None, :]).astype(BF)
    w_in = jnp.concatenate(
        [dot(w_qkv[:, i * width : (i + 1) * width], pick).astype(BF) for i in range(3)], 1
    )
    w_back = lax.dot_general(
        pick, w_out, (((0,), (0,)), ((), ())), preferred_element_type=F32
    ).astype(BF)

    limit = (counts[slide_index] - seq_index * rows).reshape(1)
    heads_shape = jax.ShapeDtypeStruct((PAIRS, rows, LANES), BF)
    mid_taken, wide_taken = rows // RATE_MID, rows // n_seq
    mid_pairs = PAIRS // RATE_MID
    placed, query, keys, values, mid_local, wide_local = pl.pallas_call(
        functools.partial(project_kernel, n_seq),
        out_shape=(
            jax.ShapeDtypeStruct((rows, width), BF),
            heads_shape,
            heads_shape,
            heads_shape,
            jax.ShapeDtypeStruct((RATE_MID, mid_pairs, 3, mid_taken, LANES), BF),
            jax.ShapeDtypeStruct((n_seq, 3, wide_taken, LANES), BF),
        ),
        in_specs=[smem, vmem, vmem, vmem],
        out_specs=(vmem,) * 6,
        compiler_params=big,
        name="project",
    )(limit, landing, arrived, w_in)

    groups = [[start + i for i in range(RATE_MID)] for start in range(0, n_seq, RATE_MID)]
    wide_qkv = exchange(wide_local, "seq")
    mid_qkv = exchange(mid_local, "seq", axis_index_groups=groups)

    pair_spec = pl.BlockSpec((1, rows, LANES), lambda i: (i, 0, 0))
    near = pl.pallas_call(
        functools.partial(near_kernel, factor),
        out_shape=jax.ShapeDtypeStruct((PAIRS, rows, LANES), F32),
        grid=(PAIRS,),
        in_specs=[pair_spec] * 3,
        out_specs=pair_spec,
        compiler_params=big,
        cost_estimate=pl.CostEstimate(
            flops=2 * HEADS * rows * rows * LANES,
            bytes_accessed=10 * rows * padded,
            transcendentals=HEADS * rows * rows // 2,
        ),
        name="near",
    )(query, keys, values)

    def far(array):
        count, pairs, _, taken, _ = array.shape
        return pl.pallas_call(
            functools.partial(far_kernel, factor),
            out_shape=jax.ShapeDtypeStruct((count, pairs, taken, LANES), BF),
            grid=(pairs,),
            in_specs=[pl.BlockSpec((count, 1, 3, taken, LANES), lambda i: (0, i, 0, 0, 0))],
            out_specs=pl.BlockSpec((count, 1, taken, LANES), lambda i: (0, i, 0, 0)),
            compiler_params=big,
            cost_estimate=pl.CostEstimate(
                flops=8 * pairs * (count * taken) ** 2 * LANES,
                bytes_accessed=8 * pairs * count * taken * LANES,
                transcendentals=2 * pairs * (count * taken) ** 2,
            ),
            name="far",
        )(array)

    wide_out = far(wide_qkv.reshape(n_seq, 1, 3, wide_taken, LANES))
    wide_back = exchange(wide_out.reshape(n_seq, wide_taken, LANES), "seq")
    mid_out = far(mid_qkv)
    mid_back = exchange(mid_out, "seq", axis_index_groups=groups)

    return pl.pallas_call(
        functools.partial(merge_kernel, n_seq),
        out_shape=jax.ShapeDtypeStruct((rows, width), BF),
        in_specs=[smem] + [vmem] * 5,
        out_specs=vmem,
        scratch_shapes=[pltpu.VMEM((PAIRS, rows, LANES), BF)],
        compiler_params=big,
        name="merge",
    )(limit, near, mid_back, wide_back, w_back, placed)


def solution(mesh):
    return jax.shard_map(
        body,
        mesh=mesh,
        in_specs=(P(("slide", "seq"), None), P(("slide", "seq")), P(), P(), P()),
        out_specs=P(("slide", "seq"), None),
        check_vma=False,
    )
```

```python
import functools
import math

import jax
import jax.numpy as jnp
from jax import lax
from jax.experimental import pallas as pl
from jax.experimental.pallas import tpu as pltpu
from jax.sharding import PartitionSpec as P

HEADS = 16
RATE_MID = 4
PAIRS = HEADS // 2
LANES = 128
NT = (((1,), (1,)), ((), ()))
BF = jnp.bfloat16
F32 = jnp.float32


def iota(shape, dim):
    return lax.broadcasted_iota(jnp.int32, shape, dim)


def dot(a, b):
    return jnp.dot(a, b, preferred_element_type=F32)


def dot_nt(a, b):
    return lax.dot_general(a, b, NT, preferred_element_type=F32)


def position_of(row, rows, n_seq):
    half = rows // 2
    run = half // n_seq
    seg = row // half
    block = (row % half) // run
    index = row % run
    group = n_seq // RATE_MID
    residue = (block % group) * RATE_MID + block // group
    return seg * half + index * n_seq + residue


def row_of(position, rows, n_seq):
    half = rows // 2
    run = half // n_seq
    seg = position // half
    within = position % half
    residue = within % n_seq
    block = (residue % RATE_MID) * (n_seq // RATE_MID) + residue // RATE_MID
    return seg * half + block * run + within // n_seq


def block_of(residue, n_seq):
    return (residue % RATE_MID) * (n_seq // RATE_MID) + residue // RATE_MID


def layer_norm(values):
    mean = jnp.mean(values, -1, keepdims=True)
    centred = values - mean
    var = jnp.mean(centred * centred, -1, keepdims=True)
    return centred * lax.rsqrt(var + 1e-05)


def dispatch_kernel(owners, most, n_seq, route_ref, tiles_ref, out_ref):
    rows = tiles_ref.shape[0]
    slots = owners * most
    target = route_ref[...] // rows
    mine = iota((owners, rows), 0) == target
    upper = (iota((rows, rows), 0) <= iota((rows, rows), 1)).astype(BF)
    counted = dot(mine.astype(BF), upper)
    rank = jnp.sum(jnp.where(mine, counted, 0.0), 0, keepdims=True).astype(jnp.int32) - 1
    slot = target * most + rank
    move = (iota((slots, rows), 0) == slot).astype(BF)
    width = tiles_ref.shape[1]
    out_ref[:, :width] = dot(move, tiles_ref[...]).astype(BF)
    local = row_of(route_ref[...] % rows, rows, n_seq)
    kind = iota((LANES, rows), 0)
    digits = jnp.where(
        kind == 0, local // 32, jnp.where(kind == 1, local % 32, jnp.where(kind == 2, 1, 0))
    )
    out_ref[:, width:] = dot_nt(move, digits.astype(F32).astype(BF)).astype(BF)


def project_kernel(n_seq, limit_ref, arrived_ref, w_ref, placed_ref, q_ref, k_ref,
                   v_ref, mid_ref, wide_ref):
    rows = placed_ref.shape[0]
    half = rows // 2
    run = half // n_seq
    step = half // RATE_MID
    slots = arrived_ref.shape[0]
    features = placed_ref.shape[1]
    unit = (iota((8, LANES), 0) == iota((8, LANES), 1)).astype(BF)
    sent = dot_nt(unit, arrived_ref[:, features:])
    place = sent[0:1] * 32.0 + sent[1:2] + (1.0 - sent[2:3]) * (2.0 * rows)
    take = (iota((rows, slots), 0) == place.astype(jnp.int32)).astype(BF)
    placed = dot(take, arrived_ref[:, :features])
    placed_ref[...] = placed.astype(BF)
    normed = layer_norm(placed).astype(BF)
    lane = iota((rows, 2 * LANES), 1) % LANES
    position = position_of(iota((rows, 2 * LANES), 0), rows, n_seq)
    valid = position < limit_ref[0]
    flag = (lane == 96) | (lane == 97)
    ones = jnp.where(flag, 1.0, 0.0)
    bias = jnp.where(flag & jnp.logical_not(valid), -1e30, 0.0)
    width = PAIRS * LANES
    for couple in range(0, PAIRS, 2):
        for part, (ref, extra) in enumerate(((q_ref, ones), (k_ref, bias), (v_ref, ones))):
            start = part * width + couple * LANES
            both = (dot(normed, w_ref[:, start : start + 2 * LANES]) + extra).astype(BF)
            for pair in (couple, couple + 1):
                value = both[:, (pair - couple) * LANES : (pair - couple + 1) * LANES]
                ref[pair] = value
                for seg in range(2):
                    owner = pair % RATE_MID
                    base = seg * half + owner * step
                    mid_ref[owner, pair // RATE_MID, part, seg * step : (seg + 1) * step] = (
                        value[base : base + step]
                    )
                    for residue in range(pair, n_seq, PAIRS):
                        base = seg * half + block_of(residue, n_seq) * run
                        wide_ref[residue, part, seg * run : (seg + 1) * run] = value[
                            base : base + run
                        ]


def one_head(query, keys, values, head, factor):
    lane = iota(query.shape, 1)
    own = ((lane >= 48 * head) & (lane < 48 * head + 48)) | (lane == 96 + head)
    query = jnp.where(own, query, jnp.zeros_like(query))
    scores = dot_nt(query, keys)
    top = jnp.max(scores, -1, keepdims=True)
    weights = jnp.exp2((scores - top) * factor).astype(BF)
    result = dot(weights, values)
    total = result[:, 96:97]
    return result * (1.0 / total), top * factor + jnp.log2(total)


def near_kernel(factor, q_ref, k_ref, v_ref, out_ref):
    rows = q_ref.shape[1]
    half = rows // 2
    block = 256
    for seg in range(2):
        keys = k_ref[0, seg * half : (seg + 1) * half]
        values = v_ref[0, seg * half : (seg + 1) * half]
        for start in range(seg * half, (seg + 1) * half, block):
            query = q_ref[0, start : start + block]
            result_a, log_a = one_head(query, keys, values, 0, factor)
            result_b, log_b = one_head(query, keys, values, 1, factor)
            lane = iota(result_a.shape, 1)
            packed = jnp.where(lane < 48, result_a, result_b)
            packed = jnp.where(lane == 96, log_a, packed)
            packed = jnp.where(lane == 97, log_b, packed)
            out_ref[0, start : start + block] = packed


def pieces(value):
    first = value.astype(BF).astype(F32)
    second = (value - first).astype(BF).astype(F32)
    return first, second, value - first - second


def far_kernel(factor, ref, out_ref):
    count, taken = ref.shape[0], ref.shape[3]
    total = count * taken
    keys = ref[:, 0, 1].reshape(total, LANES)
    values = ref[:, 0, 2].reshape(total, LANES)
    for source in range(count):
        query = ref[source, 0, 0]
        result_a, log_a = one_head(query, keys, values, 0, factor)
        result_b, log_b = one_head(query, keys, values, 1, factor)
        lane = iota(result_a.shape, 1)
        packed = jnp.where(lane < 48, result_a, result_b)
        for index, piece in enumerate(pieces(log_a) + pieces(log_b)):
            packed = jnp.where(lane == 96 + index, piece, packed)
        out_ref[source, 0] = packed.astype(BF)


def merge_kernel(n_seq, limit_ref, first_ref, second_ref, third_ref, mid_ref, wide_ref, w_ref,
                 placed_ref, out_ref, att_ref):
    rows = placed_ref.shape[0]
    half = rows // 2
    run = half // n_seq
    step = half // RATE_MID
    group = n_seq // RATE_MID

    def log_of(packed, head):
        at = 96 + 3 * head
        return packed[:, at : at + 1] + packed[:, at + 1 : at + 2] + packed[:, at + 2 : at + 3]

    for pair in range(PAIRS):
        if pair < 3:
            near_ref = first_ref.at[pair]
        elif pair < 6:
            near_ref = second_ref.at[pair - 3]
        else:
            near_ref = third_ref.at[pair - 6]
        near_all = near_ref[...]
        lane = iota(near_all.shape, 1)
        att_ref[pair] = jnp.where(lane < 96, near_all, 0.0).astype(BF)
        mid_all = mid_ref[pair % RATE_MID, pair // RATE_MID].astype(F32)
        lane = iota((run, LANES), 1)
        for seg in range(2):
            base = seg * half + (pair % RATE_MID) * step
            for index in range(group):
                part = slice(base + index * run, base + (index + 1) * run)
                near = near_ref[part]
                at = seg * step + index * run
                mid = mid_all[at : at + run]
                merged = []
                for head in range(2):
                    residue = (pair + head * PAIRS) % n_seq
                    log_near, log_mid = near[:, 96 + head : 97 + head], log_of(mid, head)
                    top = jnp.maximum(log_near, log_mid)
                    has_wide = residue // RATE_MID == index
                    if has_wide:
                        wide = wide_ref[residue, seg * run : (seg + 1) * run].astype(F32)
                        log_wide = log_of(wide, head)
                        top = jnp.maximum(top, log_wide)
                    weight_near, weight_mid = jnp.exp2(log_near - top), jnp.exp2(log_mid - top)
                    numer = near * weight_near + mid * weight_mid
                    denom = weight_near + weight_mid
                    if has_wide:
                        weight_wide = jnp.exp2(log_wide - top)
                        numer += wide * weight_wide
                        denom += weight_wide
                    merged.append(numer * (1.0 / denom))
                both = jnp.where(lane < 48, merged[0], jnp.where(lane < 96, merged[1], 0.0))
                att_ref[pair, part] = both.astype(BF)

    limit = limit_ref[0]
    unsort = (row_of(iota((half, half), 0), rows, n_seq) == iota((half, half), 1)).astype(BF)
    for seg in range(2):
        part = slice(seg * half, (seg + 1) * half)
        attended = jnp.concatenate([att_ref[pair, part] for pair in range(PAIRS)], 1)
        projected = dot(attended, w_ref[...])
        mixed = placed_ref[part].astype(F32) + layer_norm(projected)
        position = iota(mixed.shape, 0) + seg * half
        mixed = dot(unsort, mixed.astype(BF))
        out_ref[part] = jnp.where(position < limit, mixed, 0.0).astype(BF)


def body(tiles, route, counts, w_qkv, w_out):
    rows, width = tiles.shape
    n_slide = lax.axis_size("slide")
    n_seq = lax.axis_size("seq")
    owners = n_slide * n_seq
    most = 3 * rows // (2 * owners)
    slots = owners * most
    head_dim = width // HEADS
    factor = math.log2(math.e) / math.sqrt(head_dim)
    padded = PAIRS * LANES
    vmem = pl.BlockSpec(memory_space=pltpu.VMEM)
    smem = pl.BlockSpec(memory_space=pltpu.SMEM)
    big = pltpu.CompilerParams(vmem_limit_bytes=48 << 20)

    seq_index = lax.axis_index("seq")
    slide_index = lax.axis_index("slide")
    both_axes = ("slide", "seq")
    outgoing = pl.pallas_call(
        functools.partial(dispatch_kernel, owners, most, n_seq),
        out_shape=jax.ShapeDtypeStruct((slots, width + LANES), BF),
        in_specs=[vmem, vmem],
        out_specs=vmem,
        compiler_params=big,
        name="dispatch",
    )(route.reshape(1, rows), tiles)
    exchange = functools.partial(lax.all_to_all, split_axis=0, concat_axis=0, tiled=True)
    sent_width = width + LANES
    arrived = exchange(outgoing.reshape(owners, most, sent_width), both_axes)
    arrived = arrived.reshape(slots, sent_width)

    column = jnp.arange(padded)
    lane = column % LANES
    source = (column // LANES + PAIRS * (lane // head_dim)) * head_dim + lane % head_dim
    source = jnp.where(lane < 2 * head_dim, source, -1)
    pick = (jnp.arange(width)[:, None] == source[None, :]).astype(BF)
    w_in = jnp.concatenate(
        [dot(w_qkv[:, i * width : (i + 1) * width], pick).astype(BF) for i in range(3)], 1
    )
    w_back = lax.dot_general(
        pick, w_out, (((0,), (0,)), ((), ())), preferred_element_type=F32
    ).astype(BF)

    limit = (counts[slide_index] - seq_index * rows).reshape(1)
    heads_shape = jax.ShapeDtypeStruct((PAIRS, rows, LANES), BF)
    mid_taken, wide_taken = rows // RATE_MID, rows // n_seq
    mid_pairs = PAIRS // RATE_MID
    placed, query, keys, values, mid_local, wide_local = pl.pallas_call(
        functools.partial(project_kernel, n_seq),
        out_shape=(
            jax.ShapeDtypeStruct((rows, width), BF),
            heads_shape,
            heads_shape,
            heads_shape,
            jax.ShapeDtypeStruct((RATE_MID, mid_pairs, 3, mid_taken, LANES), BF),
            jax.ShapeDtypeStruct((n_seq, 3, wide_taken, LANES), BF),
        ),
        in_specs=[smem, vmem, vmem],
        out_specs=(vmem,) * 6,
        compiler_params=big,
        name="project",
    )(limit, arrived, w_in)

    groups = [[start + i for i in range(RATE_MID)] for start in range(0, n_seq, RATE_MID)]
    wide_qkv = exchange(wide_local, "seq")
    def near(first, count):
        spec = pl.BlockSpec((1, rows, LANES), lambda i: (i + first, 0, 0))
        return pl.pallas_call(
            functools.partial(near_kernel, factor),
            out_shape=jax.ShapeDtypeStruct((count, rows, LANES), F32),
            grid=(count,),
            in_specs=[spec] * 3,
            out_specs=pl.BlockSpec((1, rows, LANES), lambda i: (i, 0, 0)),
            compiler_params=big,
            cost_estimate=pl.CostEstimate(
                flops=4 * count * rows * rows * LANES,
                bytes_accessed=10 * rows * LANES * count,
                transcendentals=count * rows * rows,
            ),
            name="near",
        )(query, keys, values)

    near_first, near_second, near_third = near(0, 3), near(3, 3), near(6, 2)

    def far(array):
        count, pairs, _, taken, _ = array.shape
        return pl.pallas_call(
            functools.partial(far_kernel, factor),
            out_shape=jax.ShapeDtypeStruct((count, pairs, taken, LANES), BF),
            grid=(pairs,),
            in_specs=[pl.BlockSpec((count, 1, 3, taken, LANES), lambda i: (0, i, 0, 0, 0))],
            out_specs=pl.BlockSpec((count, 1, taken, LANES), lambda i: (0, i, 0, 0)),
            compiler_params=big,
            cost_estimate=pl.CostEstimate(
                flops=8 * pairs * (count * taken) ** 2 * LANES,
                bytes_accessed=8 * pairs * count * taken * LANES,
                transcendentals=2 * pairs * (count * taken) ** 2,
            ),
            name="far",
        )(array)

    wide_qkv, mid_local, near_first = lax.optimization_barrier((wide_qkv, mid_local, near_first))
    mid_qkv = exchange(mid_local, "seq", axis_index_groups=groups)
    wide_out = far(wide_qkv.reshape(n_seq, 1, 3, wide_taken, LANES))
    wide_out, near_second = lax.optimization_barrier((wide_out, near_second))
    wide_back = exchange(wide_out.reshape(n_seq, wide_taken, LANES), "seq")
    mid_out = far(mid_qkv)
    mid_back = exchange(mid_out, "seq", axis_index_groups=groups)

    return pl.pallas_call(
        functools.partial(merge_kernel, n_seq),
        out_shape=jax.ShapeDtypeStruct((rows, width), BF),
        in_specs=[smem] + [vmem] * 7,
        out_specs=vmem,
        scratch_shapes=[pltpu.VMEM((PAIRS, rows, LANES), BF)],
        compiler_params=big,
        name="merge",
    )(limit, near_first, near_second, near_third, mid_back, wide_back, w_back, placed)


def solution(mesh):
    return jax.shard_map(
        body,
        mesh=mesh,
        in_specs=(P(("slide", "seq"), None), P(("slide", "seq")), P(), P(), P()),
        out_specs=P(("slide", "seq"), None),
        check_vma=False,
    )
```

```python
import functools
import math

import jax
import jax.numpy as jnp
from jax import lax
from jax.experimental import pallas as pl
from jax.experimental.pallas import tpu as pltpu
from jax.sharding import PartitionSpec as P

HEADS = 16
RATE_MID = 4
PAIRS = HEADS // 2
LANES = 128
NT = (((1,), (1,)), ((), ()))
BF = jnp.bfloat16
F32 = jnp.float32


def iota(shape, dim):
    return lax.broadcasted_iota(jnp.int32, shape, dim)


def dot(a, b):
    return jnp.dot(a, b, preferred_element_type=F32)


def dot_nt(a, b):
    return lax.dot_general(a, b, NT, preferred_element_type=F32)


def position_of(row, rows, n_seq):
    half = rows // 2
    run = half // n_seq
    seg = row // half
    block = (row % half) // run
    index = row % run
    group = n_seq // RATE_MID
    residue = (block % group) * RATE_MID + block // group
    return seg * half + index * n_seq + residue


def row_of(position, rows, n_seq):
    half = rows // 2
    run = half // n_seq
    seg = position // half
    within = position % half
    residue = within % n_seq
    block = (residue % RATE_MID) * (n_seq // RATE_MID) + residue // RATE_MID
    return seg * half + block * run + within // n_seq


def block_of(residue, n_seq):
    return (residue % RATE_MID) * (n_seq // RATE_MID) + residue // RATE_MID


def layer_norm(values):
    mean = jnp.mean(values, -1, keepdims=True)
    centred = values - mean
    var = jnp.mean(centred * centred, -1, keepdims=True)
    return centred * lax.rsqrt(var + 1e-05)


def dispatch_kernel(owners, most, n_seq, route_ref, tiles_ref, out_ref):
    rows = tiles_ref.shape[0]
    slots = owners * most
    target = route_ref[...] // rows
    mine = iota((owners, rows), 0) == target
    upper = (iota((rows, rows), 0) <= iota((rows, rows), 1)).astype(BF)
    counted = dot(mine.astype(BF), upper)
    rank = jnp.sum(jnp.where(mine, counted, 0.0), 0, keepdims=True).astype(jnp.int32) - 1
    slot = target * most + rank
    move = (iota((slots, rows), 0) == slot).astype(BF)
    width = tiles_ref.shape[1]
    out_ref[:, :width] = dot(move, tiles_ref[...]).astype(BF)
    local = row_of(route_ref[...] % rows, rows, n_seq)
    kind = iota((LANES, rows), 0)
    digits = jnp.where(
        kind == 0, local // 32, jnp.where(kind == 1, local % 32, jnp.where(kind == 2, 1, 0))
    )
    out_ref[:, width:] = dot_nt(move, digits.astype(F32).astype(BF)).astype(BF)


def project_kernel(n_seq, limit_ref, arrived_ref, w_ref, placed_ref, q_ref, k_ref,
                   v_ref, mid_ref, wide_ref):
    rows = placed_ref.shape[0]
    half = rows // 2
    run = half // n_seq
    step = half // RATE_MID
    slots = arrived_ref.shape[0]
    features = placed_ref.shape[1]
    unit = (iota((8, LANES), 0) == iota((8, LANES), 1)).astype(BF)
    sent = dot_nt(unit, arrived_ref[:, features:])
    place = sent[0:1] * 32.0 + sent[1:2] + (1.0 - sent[2:3]) * (2.0 * rows)
    take = (iota((rows, slots), 0) == place.astype(jnp.int32)).astype(BF)
    placed = dot(take, arrived_ref[:, :features])
    placed_ref[...] = placed.astype(BF)
    normed = layer_norm(placed).astype(BF)
    lane = iota((rows, 2 * LANES), 1) % LANES
    position = position_of(iota((rows, 2 * LANES), 0), rows, n_seq)
    valid = position < limit_ref[0]
    flag = (lane == 96) | (lane == 97)
    ones = jnp.where(flag, 1.0, 0.0)
    bias = jnp.where(flag & jnp.logical_not(valid), -1e30, 0.0)
    width = PAIRS * LANES
    for couple in range(0, PAIRS, 2):
        for part, (ref, extra) in enumerate(((q_ref, ones), (k_ref, bias), (v_ref, ones))):
            start = part * width + couple * LANES
            both = (dot(normed, w_ref[:, start : start + 2 * LANES]) + extra).astype(BF)
            for pair in (couple, couple + 1):
                value = both[:, (pair - couple) * LANES : (pair - couple + 1) * LANES]
                ref[pair] = value
                for seg in range(2):
                    owner = pair % RATE_MID
                    base = seg * half + owner * step
                    mid_ref[owner, pair // RATE_MID, part, seg * step : (seg + 1) * step] = (
                        value[base : base + step]
                    )
                    for residue in range(pair, n_seq, PAIRS):
                        base = seg * half + block_of(residue, n_seq) * run
                        wide_ref[residue, part, seg * run : (seg + 1) * run] = value[
                            base : base + run
                        ]


def one_head(query, keys, values, head, factor):
    lane = iota(query.shape, 1)
    own = ((lane >= 48 * head) & (lane < 48 * head + 48)) | (lane == 96 + head)
    query = jnp.where(own, query, jnp.zeros_like(query))
    scores = dot_nt(query, keys)
    top = jnp.max(scores, -1, keepdims=True)
    weights = jnp.exp2((scores - top) * factor).astype(BF)
    result = dot(weights, values)
    total = result[:, 96:97]
    return result * (1.0 / total), top * factor + jnp.log2(total)


def near_kernel(factor, q_ref, k_ref, v_ref, out_ref):
    rows = q_ref.shape[1]
    half = rows // 2
    block = 256
    for seg in range(2):
        keys = k_ref[0, seg * half : (seg + 1) * half]
        values = v_ref[0, seg * half : (seg + 1) * half]
        for start in range(seg * half, (seg + 1) * half, block):
            query = q_ref[0, start : start + block]
            result_a, log_a = one_head(query, keys, values, 0, factor)
            result_b, log_b = one_head(query, keys, values, 1, factor)
            lane = iota(result_a.shape, 1)
            packed = jnp.where(lane < 48, result_a, result_b)
            packed = jnp.where(lane == 96, log_a, packed)
            packed = jnp.where(lane == 97, log_b, packed)
            out_ref[0, start : start + block] = packed


def pieces(value):
    first = value.astype(BF).astype(F32)
    second = (value - first).astype(BF).astype(F32)
    return first, second, value - first - second


def far_kernel(factor, ref, out_ref):
    count, taken = ref.shape[0], ref.shape[3]
    total = count * taken
    keys = ref[:, 0, 1].reshape(total, LANES)
    values = ref[:, 0, 2].reshape(total, LANES)
    for source in range(count):
        query = ref[source, 0, 0]
        result_a, log_a = one_head(query, keys, values, 0, factor)
        result_b, log_b = one_head(query, keys, values, 1, factor)
        lane = iota(result_a.shape, 1)
        packed = jnp.where(lane < 48, result_a, result_b)
        for index, piece in enumerate(pieces(log_a) + pieces(log_b)):
            packed = jnp.where(lane == 96 + index, piece, packed)
        out_ref[source, 0] = packed.astype(BF)


def merge_kernel(n_seq, limit_ref, first_ref, second_ref, third_ref, mid_ref, wide_ref, w_ref,
                 placed_ref, out_ref, att_ref):
    rows = placed_ref.shape[0]
    half = rows // 2
    run = half // n_seq
    step = half // RATE_MID
    group = n_seq // RATE_MID

    def log_of(packed, head):
        at = 96 + 3 * head
        return packed[:, at : at + 1] + packed[:, at + 1 : at + 2] + packed[:, at + 2 : at + 3]

    for pair in range(PAIRS):
        if pair < 4:
            near_ref = first_ref.at[pair]
        elif pair < 6:
            near_ref = second_ref.at[pair - 4]
        else:
            near_ref = third_ref.at[pair - 6]
        near_all = near_ref[...]
        lane = iota(near_all.shape, 1)
        att_ref[pair] = jnp.where(lane < 96, near_all, 0.0).astype(BF)
        mid_all = mid_ref[pair % RATE_MID, pair // RATE_MID].astype(F32)
        lane = iota((run, LANES), 1)
        for seg in range(2):
            base = seg * half + (pair % RATE_MID) * step
            for index in range(group):
                part = slice(base + index * run, base + (index + 1) * run)
                near = near_ref[part]
                at = seg * step + index * run
                mid = mid_all[at : at + run]
                merged = []
                for head in range(2):
                    residue = (pair + head * PAIRS) % n_seq
                    log_near, log_mid = near[:, 96 + head : 97 + head], log_of(mid, head)
                    top = jnp.maximum(log_near, log_mid)
                    has_wide = residue // RATE_MID == index
                    if has_wide:
                        wide = wide_ref[residue, seg * run : (seg + 1) * run].astype(F32)
                        log_wide = log_of(wide, head)
                        top = jnp.maximum(top, log_wide)
                    weight_near, weight_mid = jnp.exp2(log_near - top), jnp.exp2(log_mid - top)
                    numer = near * weight_near + mid * weight_mid
                    denom = weight_near + weight_mid
                    if has_wide:
                        weight_wide = jnp.exp2(log_wide - top)
                        numer += wide * weight_wide
                        denom += weight_wide
                    merged.append(numer * (1.0 / denom))
                both = jnp.where(lane < 48, merged[0], jnp.where(lane < 96, merged[1], 0.0))
                att_ref[pair, part] = both.astype(BF)

    limit = limit_ref[0]
    unsort = (row_of(iota((half, half), 0), rows, n_seq) == iota((half, half), 1)).astype(BF)
    for seg in range(2):
        part = slice(seg * half, (seg + 1) * half)
        attended = jnp.concatenate([att_ref[pair, part] for pair in range(PAIRS)], 1)
        projected = dot(attended, w_ref[...])
        mixed = placed_ref[part].astype(F32) + layer_norm(projected)
        position = iota(mixed.shape, 0) + seg * half
        mixed = dot(unsort, mixed.astype(BF))
        out_ref[part] = jnp.where(position < limit, mixed, 0.0).astype(BF)


def body(tiles, route, counts, w_qkv, w_out):
    rows, width = tiles.shape
    n_slide = lax.axis_size("slide")
    n_seq = lax.axis_size("seq")
    owners = n_slide * n_seq
    most = 3 * rows // (2 * owners)
    slots = owners * most
    head_dim = width // HEADS
    factor = math.log2(math.e) / math.sqrt(head_dim)
    padded = PAIRS * LANES
    vmem = pl.BlockSpec(memory_space=pltpu.VMEM)
    smem = pl.BlockSpec(memory_space=pltpu.SMEM)
    big = pltpu.CompilerParams(vmem_limit_bytes=48 << 20)

    seq_index = lax.axis_index("seq")
    slide_index = lax.axis_index("slide")
    both_axes = ("slide", "seq")
    outgoing = pl.pallas_call(
        functools.partial(dispatch_kernel, owners, most, n_seq),
        out_shape=jax.ShapeDtypeStruct((slots, width + LANES), BF),
        in_specs=[vmem, vmem],
        out_specs=vmem,
        compiler_params=big,
        name="dispatch",
    )(route.reshape(1, rows), tiles)
    exchange = functools.partial(lax.all_to_all, split_axis=0, concat_axis=0, tiled=True)
    sent_width = width + LANES
    arrived = exchange(outgoing.reshape(owners, most, sent_width), both_axes)
    arrived = arrived.reshape(slots, sent_width)

    column = jnp.arange(padded)
    lane = column % LANES
    source = (column // LANES + PAIRS * (lane // head_dim)) * head_dim + lane % head_dim
    source = jnp.where(lane < 2 * head_dim, source, -1)
    pick = (jnp.arange(width)[:, None] == source[None, :]).astype(BF)
    w_in = jnp.concatenate(
        [dot(w_qkv[:, i * width : (i + 1) * width], pick).astype(BF) for i in range(3)], 1
    )
    w_back = lax.dot_general(
        pick, w_out, (((0,), (0,)), ((), ())), preferred_element_type=F32
    ).astype(BF)

    limit = (counts[slide_index] - seq_index * rows).reshape(1)
    heads_shape = jax.ShapeDtypeStruct((PAIRS, rows, LANES), BF)
    mid_taken, wide_taken = rows // RATE_MID, rows // n_seq
    mid_pairs = PAIRS // RATE_MID
    placed, query, keys, values, mid_local, wide_local = pl.pallas_call(
        functools.partial(project_kernel, n_seq),
        out_shape=(
            jax.ShapeDtypeStruct((rows, width), BF),
            heads_shape,
            heads_shape,
            heads_shape,
            jax.ShapeDtypeStruct((RATE_MID, mid_pairs, 3, mid_taken, LANES), BF),
            jax.ShapeDtypeStruct((n_seq, 3, wide_taken, LANES), BF),
        ),
        in_specs=[smem, vmem, vmem],
        out_specs=(vmem,) * 6,
        compiler_params=big,
        name="project",
    )(limit, arrived, w_in)

    groups = [[start + i for i in range(RATE_MID)] for start in range(0, n_seq, RATE_MID)]
    wide_qkv = exchange(wide_local, "seq")
    def near(first, count):
        spec = pl.BlockSpec((1, rows, LANES), lambda i: (i + first, 0, 0))
        return pl.pallas_call(
            functools.partial(near_kernel, factor),
            out_shape=jax.ShapeDtypeStruct((count, rows, LANES), F32),
            grid=(count,),
            in_specs=[spec] * 3,
            out_specs=pl.BlockSpec((1, rows, LANES), lambda i: (i, 0, 0)),
            compiler_params=big,
            cost_estimate=pl.CostEstimate(
                flops=4 * count * rows * rows * LANES,
                bytes_accessed=10 * rows * LANES * count,
                transcendentals=count * rows * rows,
            ),
            name="near",
        )(query, keys, values)

    near_first, near_second, near_third = near(0, 4), near(4, 2), near(6, 2)

    def far(array):
        count, pairs, _, taken, _ = array.shape
        return pl.pallas_call(
            functools.partial(far_kernel, factor),
            out_shape=jax.ShapeDtypeStruct((count, pairs, taken, LANES), BF),
            grid=(pairs,),
            in_specs=[pl.BlockSpec((count, 1, 3, taken, LANES), lambda i: (0, i, 0, 0, 0))],
            out_specs=pl.BlockSpec((count, 1, taken, LANES), lambda i: (0, i, 0, 0)),
            compiler_params=big,
            cost_estimate=pl.CostEstimate(
                flops=8 * pairs * (count * taken) ** 2 * LANES,
                bytes_accessed=8 * pairs * count * taken * LANES,
                transcendentals=2 * pairs * (count * taken) ** 2,
            ),
            name="far",
        )(array)

    wide_qkv, mid_local, near_first = lax.optimization_barrier((wide_qkv, mid_local, near_first))
    mid_qkv = exchange(mid_local, "seq", axis_index_groups=groups)
    wide_out = far(wide_qkv.reshape(n_seq, 1, 3, wide_taken, LANES))
    wide_out, near_second = lax.optimization_barrier((wide_out, near_second))
    wide_back = exchange(wide_out.reshape(n_seq, wide_taken, LANES), "seq")
    mid_out = far(mid_qkv)
    mid_back = exchange(mid_out, "seq", axis_index_groups=groups)

    return pl.pallas_call(
        functools.partial(merge_kernel, n_seq),
        out_shape=jax.ShapeDtypeStruct((rows, width), BF),
        in_specs=[smem] + [vmem] * 7,
        out_specs=vmem,
        scratch_shapes=[pltpu.VMEM((PAIRS, rows, LANES), BF)],
        compiler_params=big,
        name="merge",
    )(limit, near_first, near_second, near_third, mid_back, wide_back, w_back, placed)


def solution(mesh):
    return jax.shard_map(
        body,
        mesh=mesh,
        in_specs=(P(("slide", "seq"), None), P(("slide", "seq")), P(), P(), P()),
        out_specs=P(("slide", "seq"), None),
        check_vma=False,
    )
```
